1024 devices in a mesh: section: 8 (over y, z_hi), dp: 4 (over x), tensor: 32 (over z_lo, core).
Axes of the slice: x: 4, y: 4, z: 32 (z_hi: 2, z_lo: 16; z = z_hi * 16 + z_lo), core: 2. Of those that a mesh axis runs over, the one named last changes fastest.
Arguments:
- cache: bfloat16 [8, 256, 5376], P('section'), may hold values from -6 to 6
- token_ids: int32 [128], replicated, may hold values from 0 to 255
- enc_weight: bfloat16 [8, 8192, 5376], P('section', ('dp', 'tensor')), may hold values from -0.078125 to 0.078125
- enc_bias: float32 [8, 8192], P('section', ('dp', 'tensor')), may hold values from -3 to 3
- dec_weight: bfloat16 [8, 8, 2688, 8192], P('section', None, ('dp', 'tensor')), may hold values from -0.25 to 0.25
- dec_bias: float32 [8, 2688], P('section', ('dp', 'tensor')), may hold values from -3 to 3
- incoming: float32 [8, 128, 2688], P('section', None, ('dp', 'tensor')), may hold values from -6 to 6
- target: bfloat16 [8, 128, 2688], P('section', None, ('dp', 'tensor')), may hold values from -6 to 6
- returned: bfloat16 [8, 128, 2688], P('section', None, ('dp', 'tensor')), may hold values from -6 to 6
Outputs:
- error: bfloat16 [8, 128, 2688], P('section', None, ('dp', 'tensor'))
- outgoing: float32 [8, 128, 2688], P('section', None, ('dp', 'tensor'))
- lat_grad: float32 [8, 8192, 128], P('section', ('dp', 'tensor'))
The draws below stay inside these ranges and needn't reach their ends.
All inputs are finite; a program needn't handle non-finite values.
Results may differ from the reference program's by a relative error of at most 0.014.
Values may be sent and summed in bfloat16 or wider, within the bound.
A program may use at most 64 MiB of HBM per device.

```python
import jax
import jax.numpy as jnp

D = 5376
LAT = 8192
DO = 2688
TOKENS = 128
LAYERS = 8
CACHE_ROWS = 256


def touch_ends(array, stream_key, least, top_value):
    longest = array.shape.index(max(array.shape))
    spots = []
    for shift in (0, 1):
        where = [jax.random.randint(jax.random.fold_in(stream_key, axis), (), 0, length) for axis, length in enumerate(array.shape)]
        where[longest] = (where[longest] + shift) % array.shape[longest]
        spots.append(tuple(where))
    return array.at[spots[0]].set(least).at[spots[1]].set(top_value)


def spiked(values, own_key, source, target, blocks, factor):
    owner, partner = [(jnp.arange(values.shape[axis_at]) // (values.shape[axis_at] // blocks)).reshape([-1 if axis == axis_at else 1 for axis in range(values.ndim)]) for axis_at in (source, target)]
    chosen = jax.random.permutation(own_key, blocks)[partner]
    strong = (owner == chosen) | (owner == (partner + blocks // 2) % blocks)
    return jnp.where(strong, factor * values, values)


def block_scale(own_key, extent, cuts, least, largest):
    def one(dim, parts):
        steps = jax.random.uniform(jax.random.fold_in(jax.random.fold_in(own_key, 6), dim), (parts,), jnp.float32, least / len(cuts), largest / len(cuts))
        return jnp.repeat(jnp.exp(steps), extent[dim] // parts).reshape((-1,) + (1,) * (len(extent) - dim - 1))

    level = one(*cuts[0])
    for cut in cuts[1:]:
        level = level * one(*cut)
    return level


def scatter_about(stream_key, dims, width, most, cuts=(), dtype=jnp.bfloat16):
    drawn = jax.random.normal(stream_key, dims, jnp.float32) * width
    if len(cuts) > 0:
        drawn = block_scale(stream_key, dims, cuts, -0.22, 0.18) * drawn
    return jnp.clip(drawn, min=-most, max=most).astype(dtype)


def gaussian_with(key, shape, spread, limit, shards, heavy, dtype=jnp.bfloat16):
    values = spread * jax.random.normal(key, shape, jnp.float32)
    if shards:
        values = values * block_scale(key, shape, shards, -0.22, 0.18)
    return jnp.clip(spiked(values, jax.random.fold_in(key, 3), *heavy), -limit, limit).astype(dtype)


def setup_inputs(seed: int = 0) -> dict:
    key_of = jax.random.split(jax.random.key(seed), 10)
    return {
        "cache": scatter_about(key_of[0], (LAYERS, CACHE_ROWS, D), 1.0, 6.0, ((0, 8),)),
        "token_ids": touch_ends(jax.random.randint(key_of[1], (TOKENS,), 0, CACHE_ROWS), jax.random.fold_in(key_of[1], 1), 0, CACHE_ROWS - 1).astype(jnp.int32),
        "enc_weight": scatter_about(key_of[2], (LAYERS, LAT, D), D ** -0.5, 0.078125, ((0, 8), (1, 128))),
        "enc_bias": scatter_about(key_of[3], (LAYERS, LAT), 0.5, 3.0, ((0, 8), (1, 128)), jnp.float32),
        "dec_weight": gaussian_with(key_of[4], (LAYERS, LAYERS, DO, LAT), LAT ** -0.5, 0.25, ((0, 8), (2, 128)), (3, 2, 128, 5.5)),
        "dec_bias": scatter_about(key_of[5], (LAYERS, DO), 0.5, 3.0, ((0, 8), (1, 128)), jnp.float32),
        "incoming": scatter_about(key_of[6], (LAYERS, TOKENS, DO), 1.0, 6.0, ((0, 8), (2, 128)), jnp.float32),
        "target": scatter_about(key_of[7], (LAYERS, TOKENS, DO), 1.0, 6.0, ((0, 8), (2, 128))),
        "returned": scatter_about(key_of[8], (LAYERS, TOKENS, DO), 1.0, 6.0, ((0, 8), (2, 128))),
    }


def reference(cache, token_ids, enc_weight, enc_bias, dec_weight, dec_bias, incoming, target, returned):
    layers = cache.shape[0]
    latent_list = []
    for layer in range(layers):
        rows = cache[layer][token_ids]
        pre = jnp.dot(rows, enc_weight[layer].T, preferred_element_type=jnp.float32) + enc_bias[layer]
        latent_list.append(jnp.maximum(pre, 0.0).astype(jnp.bfloat16))
    recon = [incoming[layer] + dec_bias[layer] for layer in range(layers)]
    outgo = [jnp.zeros(incoming.shape[1:], jnp.float32) for layer in range(layers)]
    for layer in range(layers):
        for offset in range(layers):
            part = jnp.dot(latent_list[layer], dec_weight[layer, offset].T, preferred_element_type=jnp.float32)
            where_to = layer + offset
            if where_to < layers:
                recon[where_to] = recon[where_to] + part
            else:
                outgo[where_to - layers] = outgo[where_to - layers] + part
    error = jnp.stack([recon[t] - target[t].astype(jnp.float32) for t in range(layers)]).astype(jnp.bfloat16)
    outgoing = jnp.stack(outgo)
    grads = []
    for layer in range(layers):
        total = jnp.zeros((dec_weight.shape[3], incoming.shape[1]), jnp.float32)
        for offset in range(layers):
            where_to = layer + offset
            if where_to < layers:
                upstream = error[where_to]
            else:
                upstream = returned[where_to - layers]
            total = total + jnp.dot(dec_weight[layer, offset].T, upstream.T, preferred_element_type=jnp.float32)
        grads.append(total)
    return error, outgoing, jnp.stack(grads)
```

```python
import functools

import jax
import jax.numpy as jnp
from jax import lax
from jax.experimental import pallas as pl
from jax.experimental.pallas import tpu as pltpu
from jax.sharding import PartitionSpec as P

MESH = pl.DeviceIdType.MESH
F32 = jnp.float32
BF16 = jnp.bfloat16
FEAT = 24
ORDER = (1, 3, 2)


class Links:
    def __init__(self, send, recv):
        self.send, self.recv, self.used, self.open = send, recv, 0, []

    def message(self):
        self.used += 1
        return self.used - 1

    def copy(self, index, src, dst, peer):
        return pltpu.make_async_remote_copy(
            src_ref=src,
            dst_ref=dst,
            send_sem=self.send.at[index],
            recv_sem=self.recv.at[index],
            device_id=peer,
            device_id_type=MESH,
        )

    def start(self, index, src, dst, peer):
        copy = self.copy(index, src, dst, peer)
        copy.start()
        self.open.append(copy)

    def arrived(self, index, dst, peer):
        self.copy(index, dst, dst, peer).wait_recv()

    def drain(self):
        for copy in self.open:
            copy.wait_send()


MESSAGES = 112


def column_of(row, rows):
    n = row.shape[1]
    down = lax.broadcasted_iota(jnp.int32, (rows, n), 0)
    along = lax.broadcasted_iota(jnp.int32, (rows, n), 1)
    return jnp.sum(jnp.where(down == along, row, 0.0), axis=1, keepdims=True)


def kernel(
    tok, ebias, dbias, inc, tgt, ret, cache_h, enc_h, w_h,
    err_o, out_o, lg_o,
    cache_v, enc_v, w_v, lat, pbuf, rc, qbuf, rx, ub, rb, vf, vb, ra,
    cacc, bk, ysend, yrecv, zsend, zrecv, osend, orecv, esend, erecv,
    rsend, rrecv, gsend, grecv, load, send, recv,
):
    s, d, t = lax.axis_index("section"), lax.axis_index("dp"), lax.axis_index("tensor")
    y, zh, x, z, c = s // 2, s % 2, d, t // 2, t % 2
    zg, zp = z // 4, z % 4
    core_peer = (s, d, z * 2 + 1 - c)
    x_peer = lambda k: (s, (x + k) % 4, t)
    a_peer = lambda k: (s, d, (((zg + k) % 4) * 4 + zp) * 2 + c)
    b_peer = lambda k: (s, d, (zg * 4 + (zp + k) % 4) * 2 + c)
    y_peer = lambda k: (((y + k) % 4) * 2 + zh, d, t)
    z_peer = (y * 2 + 1 - zh, d, t)

    barrier = pltpu.get_barrier_semaphore()
    peers = [z_peer, core_peer]
    for k in (1, 2, 3):
        peers += [a_peer(k), b_peer(k), x_peer(k), y_peer(k)]
    for peer in peers:
        pl.semaphore_signal(barrier, inc=1, device_id=peer, device_id_type=MESH)

    loads = [
        pltpu.make_async_copy(cache_h, cache_v, load.at[0]),
        pltpu.make_async_copy(enc_h, enc_v, load.at[1]),
        pltpu.make_async_copy(w_h, w_v, load.at[2]),
    ]
    for one in loads:
        one.start()
    links = Links(send, recv)

    rows_of = lax.broadcasted_iota(jnp.int32, (256, 128), 0)
    pick = jnp.where(rows_of == tok[...], 1.0, 0.0).astype(BF16)
    bias = column_of(ebias[...], 64)
    loads[0].wait()
    loads[1].wait()
    pre = lax.dot_general(
        enc_v[...], cache_v[...], (((1,), (1,)), ((), ())), preferred_element_type=F32
    )
    every = jnp.maximum(pre + bias, 0.0).astype(BF16)
    mine = jnp.dot(every, pick, preferred_element_type=F32).astype(BF16)
    lat[x, zp, zg, c] = mine

    pl.semaphore_wait(barrier, len(peers))

    m_a = {k: links.message() for k in (1, 2, 3)}
    m_b = {(k, j): links.message() for k in (1, 2, 3) for j in range(4)}
    m_x = {(k, g): links.message() for k in (1, 2, 3) for g in range(4)}
    m_c = {(k, g): links.message() for k in range(4) for g in range(4)}
    for k in ORDER:
        here = lat.at[x, zp, zg, c]
        links.start(m_a[k], here, here, a_peer(k))
    for k in ORDER:
        here = lat.at[x, zp, zg, c]
        links.start(m_b[k, 0], here, here, b_peer(k))

    zero_rows = jnp.zeros((FEAT - 21, 128), F32)
    returned = jnp.concatenate([ret[...].astype(F32), zero_rows], axis=0)
    rsend[...] = jnp.concatenate([returned, jnp.zeros((8, 128), F32)], axis=0).astype(BF16)
    m_r = links.message()
    links.start(m_r, rsend, rrecv, z_peer)

    for j in ORDER:
        from_a = lat.at[x, zp, (zg - j + 4) % 4, c]
        links.arrived(m_a[j], from_a, a_peer(j))
        for k in ORDER:
            links.start(m_b[k, j], from_a, from_a, b_peer(k))

    def group(k, g):
        return lat.at[(x - k + 4) % 4, (zp - g + 4) % 4, :, c]

    def pass_on(g):
        for k in ORDER:
            links.start(m_x[k, g], group(0, g), group(0, g), x_peer(k))
        links.start(m_c[0, g], group(0, g), group(0, g), core_peer)

    def weights(x_at, zp_at):
        cut = []
        for q in range(4):
            first = pl.multiple_of((x_at * 16 + q * 4 + zp_at) * 128, 128)
            cut.append(w_v[:, pl.ds(first, 128)])
        return jnp.concatenate(cut, axis=1)

    def decode(k, g):
        x_at, zp_at = (x - k + 4) % 4, (zp - g + 4) % 4
        links.arrived(m_c[k, g], lat.at[x_at, zp_at, :, 1 - c], core_peer)
        block = lat[x_at, zp_at].reshape(512, 128)
        cacc[0:168] += jnp.dot(weights(x_at, zp_at), block, preferred_element_type=F32)

    cacc[...] = jnp.zeros_like(cacc)
    loads[2].wait()
    sequence = (0,) + ORDER
    done = []
    for at, g in enumerate(sequence):
        if g > 0:
            for j in range(4):
                from_b = lat.at[x, (zp - g + 4) % 4, (zg - j + 4) % 4, c]
                links.arrived(m_b[g, j], from_b, b_peer(g))
        pass_on(g)
        if at > 0:
            before = sequence[at - 1]
            for k in ORDER:
                links.arrived(m_x[k, before], group(k, before), x_peer(k))
                links.start(m_c[k, before], group(k, before), group(k, before), core_peer)
            if at > 1:
                for k in range(4):
                    decode(k, sequence[at - 2])
    last = sequence[3]
    for k in range(4):
        decode(k, sequence[2])
    decode(0, last)
    for k in ORDER:
        links.arrived(m_x[k, last], group(k, last), x_peer(k))
        links.start(m_c[k, last], group(k, last), group(k, last), core_peer)

    links.arrived(m_r, rrecv, z_peer)
    gsend[...] = jnp.concatenate([returned, rrecv[...].astype(F32)[:FEAT]], axis=0).astype(BF16)
    m_g = {k: links.message() for k in (1, 2, 3)}
    for k in ORDER:
        links.start(m_g[k], gsend, grecv.at[k - 1], y_peer(k))
    for k in ORDER:
        decode(k, last)

    def piece(offset):
        return cacc[pl.ds(offset, FEAT, stride=8), :]

    cross_of = lambda dy: (2 * dy + 1 - 2 * zh + 8) % 8
    m_y = {k: links.message() for k in (1, 2, 3)}
    for k in ORDER:
        ysend[k - 1] = jnp.concatenate([piece(2 * k), piece(cross_of(k))], axis=0).astype(BF16)
        links.start(m_y[k], ysend.at[k - 1], yrecv.at[k - 1], y_peer(k))
    base = inc[...].reshape(21, 128) + column_of(dbias[...], 21) - tgt[...].astype(F32)
    base = jnp.concatenate([base, zero_rows], axis=0)
    own_cross = piece(cross_of(0))
    e_same = base + piece(0)
    o_same = jnp.zeros((FEAT, 128), F32)
    e_cross = jnp.where(zh == 0, own_cross, 0.0)
    o_cross = jnp.where(zh == 0, 0.0, own_cross)
    for k in ORDER:
        links.arrived(m_y[k], yrecv.at[k - 1], y_peer(k))
        both = yrecv[k - 1].astype(F32)
        same, cross = both[:FEAT], both[FEAT:]
        e_same += jnp.where(y >= k, same, 0.0)
        o_same += jnp.where(y >= k, 0.0, same)
        e_cross += jnp.where(y >= k, cross, 0.0)
        o_cross += jnp.where(y >= k, 0.0, cross)
    m_z, m_o = links.message(), links.message()
    zsend[...] = jnp.concatenate([e_same, e_cross], axis=0).astype(BF16)
    links.start(m_z, zsend, zrecv, z_peer)
    osend[...] = jnp.concatenate([o_cross, jnp.zeros((8, 128), F32)], axis=0).astype(BF16)
    links.start(m_o, osend, orecv, z_peer)
    links.arrived(m_z, zrecv, z_peer)
    both = zrecv[...].astype(F32)
    mine_err = e_same + both[FEAT:]
    other_err = e_cross + both[:FEAT]
    esend[...] = jnp.concatenate([mine_err, other_err], axis=0).astype(BF16)
    m_e = {k: links.message() for k in (1, 2, 3)}
    for k in ORDER:
        links.start(m_e[k], esend, erecv.at[k - 1], y_peer(k))
    err_o[...] = mine_err[:21].astype(BF16)

    for dy in range(4):
        k = (4 - dy) % 4
        if k == 0:
            mine_b, ret_b = esend[...].astype(F32), gsend[...].astype(F32)
            same = mine_b[:FEAT]
            cross = jnp.where(zh == 0, mine_b[FEAT:], ret_b[FEAT:])
        else:
            links.arrived(m_g[k], grecv.at[k - 1], y_peer(k))
            links.arrived(m_e[k], erecv.at[k - 1], y_peer(k))
            mine_b, ret_b = erecv[k - 1].astype(F32), grecv[k - 1].astype(F32)
            both = jnp.where(y + dy < 4, mine_b, ret_b)
            same, cross = both[:FEAT], both[FEAT:]
        bk[pl.ds(2 * dy, FEAT, stride=8), :] = same
        bk[pl.ds(cross_of(dy), FEAT, stride=8), :] = cross
    back = bk[0:168].astype(BF16)

    n_c = {(k, g): links.message() for k in range(4) for g in range(4)}
    n_x = {(k, g): links.message() for k in (1, 2, 3) for g in range(4)}
    n_b = {g: links.message() for g in (1, 2, 3)}
    n_a = {j: links.message() for j in (1, 2, 3)}

    def gradient(k, g):
        x_at, zp_at = (x + k) % 4, (zp + g) % 4
        part = lax.dot_general(
            weights(x_at, zp_at), back, (((0,), (0,)), ((), ())), preferred_element_type=F32
        )
        pbuf[x_at, zp_at] = part.astype(BF16).reshape(4, 2, 64, 128)
        links.start(n_c[k, g], pbuf.at[x_at, zp_at, :, 1 - c], rc.at[k, g], core_peer)

    def chip_sum(k, g):
        x_at, zp_at = (x + k) % 4, (zp + g) % 4
        links.arrived(n_c[k, g], rc.at[k, g], core_peer)
        total = pbuf[x_at, zp_at, :, c].astype(F32) + rc[k, g].astype(F32)
        qbuf[k, g] = total.astype(BF16)
        if k > 0:
            links.start(n_x[k, g], qbuf.at[k, g], rx.at[k - 1, g], x_peer(k))

    def row_sum(g):
        total = qbuf[0, g].astype(F32)
        for k in ORDER:
            links.arrived(n_x[k, g], rx.at[k - 1, g], x_peer(k))
            total += rx[k - 1, g].astype(F32)
        if g > 0:
            ub[g - 1] = total.astype(BF16)
            links.start(n_b[g], ub.at[g - 1], rb.at[g - 1], b_peer(g))
        else:
            vf[...] = total

    steps = [(k, g) for g in ORDER + (0,) for k in ORDER + (0,)]
    for at, step in enumerate(steps):
        gradient(*step)
        if at >= 2:
            chip_sum(*steps[at - 2])
    chip_sum(*steps[-2])
    chip_sum(*steps[-1])
    links.arrived(m_o, orecv, z_peer)
    outgoing = o_same + orecv[...].astype(F32)[:FEAT]
    out_o[...] = outgoing[:21].reshape(21, 1, 128)
    for g in ORDER + (0,):
        row_sum(g)
    total = vf[...]
    for g in ORDER:
        links.arrived(n_b[g], rb.at[g - 1], b_peer(g))
        total += rb[g - 1].astype(F32)
    vf[...] = total
    vb[...] = total.astype(BF16)
    for j in ORDER:
        links.start(n_a[j], vb.at[(zg + j) % 4], ra.at[j - 1], a_peer(j))
    total = vf[zg]
    for j in ORDER:
        links.arrived(n_a[j], ra.at[j - 1], a_peer(j))
        total += ra[j - 1].astype(F32)
    lg_o[...] = total
    links.drain()


def local(cache, token_ids, enc_weight, enc_bias, dec_weight, dec_bias, incoming, target, returned):
    whole = pl.BlockSpec(memory_space=pltpu.VMEM)
    left = pl.BlockSpec(memory_space=pl.ANY)
    weights = jnp.transpose(dec_weight[0], (1, 0, 2)).reshape(168, 8192)
    err, out, grad = pl.pallas_call(
        kernel,
        out_shape=(
            jax.ShapeDtypeStruct((21, 128), BF16),
            jax.ShapeDtypeStruct((21, 1, 128), F32),
            jax.ShapeDtypeStruct((64, 128), F32),
        ),
        in_specs=[whole] * 6 + [left] * 3,
        out_specs=(whole, whole, whole),
        scratch_shapes=[
            pltpu.VMEM((256, 5376), BF16),
            pltpu.VMEM((64, 5376), BF16),
            pltpu.VMEM((168, 8192), BF16),
            pltpu.VMEM((4, 4, 4, 2, 64, 128), BF16),
            pltpu.VMEM((4, 4, 4, 2, 64, 128), BF16),
            pltpu.VMEM((4, 4, 4, 64, 128), BF16),
            pltpu.VMEM((4, 4, 4, 64, 128), BF16),
            pltpu.VMEM((3, 4, 4, 64, 128), BF16),
            pltpu.VMEM((3, 4, 64, 128), BF16),
            pltpu.VMEM((3, 4, 64, 128), BF16),
            pltpu.VMEM((4, 64, 128), F32),
            pltpu.VMEM((4, 64, 128), BF16),
            pltpu.VMEM((3, 64, 128), BF16),
            pltpu.VMEM((192, 128), F32),
            pltpu.VMEM((192, 128), F32),
            pltpu.VMEM((3, 48, 128), BF16),
            pltpu.VMEM((3, 48, 128), BF16),
            pltpu.VMEM((48, 128), BF16),
            pltpu.VMEM((48, 128), BF16),
            pltpu.VMEM((32, 128), BF16),
            pltpu.VMEM((32, 128), BF16),
            pltpu.VMEM((48, 128), BF16),
            pltpu.VMEM((3, 48, 128), BF16),
            pltpu.VMEM((32, 128), BF16),
            pltpu.VMEM((32, 128), BF16),
            pltpu.VMEM((48, 128), BF16),
            pltpu.VMEM((3, 48, 128), BF16),
            pltpu.SemaphoreType.DMA((3,)),
            pltpu.SemaphoreType.DMA((MESSAGES,)),
            pltpu.SemaphoreType.DMA((MESSAGES,)),
        ],
        compiler_params=pltpu.CompilerParams(
            collective_id=0, has_side_effects=True, vmem_limit_bytes=48 << 20
        ),
        name="transcoder",
    )(
        token_ids.reshape(1, 128),
        enc_bias,
        dec_bias,
        jnp.transpose(incoming, (2, 0, 1)),
        target[0].T,
        returned[0].T,
        cache[0],
        enc_weight[0],
        weights,
    )
    return (err.T[None], jnp.transpose(out, (1, 2, 0)), grad[None])


def solution(mesh):
    placed = (
        P("section", None, None),
        P(),
        P("section", ("dp", "tensor"), None),
        P("section", ("dp", "tensor")),
        P("section", None, ("dp", "tensor"), None),
        P("section", ("dp", "tensor")),
        P("section", None, ("dp", "tensor")),
        P("section", None, ("dp", "tensor")),
        P("section", None, ("dp", "tensor")),
    )
    return jax.shard_map(
        local,
        mesh=mesh,
        in_specs=placed,
        out_specs=(
            P("section", None, ("dp", "tensor")),
            P("section", None, ("dp", "tensor")),
            P("section", ("dp", "tensor"), None),
        ),
        check_vma=False,
    )
```

```python
import jax
import jax.numpy as jnp
from jax import lax
from jax.experimental import pallas as pl
from jax.experimental.pallas import tpu as pltpu
from jax.sharding import PartitionSpec as P

MESH = pl.DeviceIdType.MESH
F32 = jnp.float32
BF16 = jnp.bfloat16
FEAT = 24
ORDER = (1, 3, 2)


class Links:
    def __init__(self, send, recv):
        self.send, self.recv, self.used, self.open = send, recv, 0, []

    def message(self):
        self.used += 1
        return self.used - 1

    def copy(self, index, src, dst, peer, lands=None):
        return pltpu.make_async_remote_copy(
            src_ref=src,
            dst_ref=dst,
            send_sem=self.send.at[index],
            recv_sem=self.recv.at[index if lands is None else lands],
            device_id=peer,
            device_id_type=MESH,
        )

    def start(self, index, src, dst, peer, lands=None):
        copy = self.copy(index, src, dst, peer, lands)
        copy.start()
        self.open.append(copy)

    def arrived(self, index, dst, peer):
        self.copy(index, dst, dst, peer).wait_recv()

    def drain(self):
        for copy in self.open:
            copy.wait_send()


MESSAGES = 112


def column_of(row, rows):
    n = row.shape[1]
    down = lax.broadcasted_iota(jnp.int32, (rows, n), 0)
    along = lax.broadcasted_iota(jnp.int32, (rows, n), 1)
    return jnp.sum(jnp.where(down == along, row, 0.0), axis=1, keepdims=True)


def kernel(
    tok_h, ebias_h, dbias_h, inc_h, tgt_h, ret_h, cache_h, enc_h, w_h,
    err_o, out_o, lg_o, tok, ebias, dbias, inc, tgt, ret,
    cache_v, enc_v, w_v, lat, pbuf, rc, qbuf, rx, ub, rb, vf, vb, ra,
    cacc, bk, ysend, yrecv, zsend, zrecv, osend, orecv, esend, erecv,
    rsend, rrecv, gsend, grecv, load, send, recv,
):
    s, d, t = lax.axis_index("section"), lax.axis_index("dp"), lax.axis_index("tensor")
    y, zh, x, z, c = s // 2, s % 2, d, t // 2, t % 2
    zg, zp = z // 4, z % 4
    core_peer = (s, d, z * 2 + 1 - c)
    x_peer = lambda k: (s, (x + k) % 4, t)
    a_peer = lambda at: (s, d, (at * 4 + zp) * 2 + c)
    b_peer = lambda k: (s, d, (zg * 4 + (zp + k) % 4) * 2 + c)
    y_peer = lambda k: (((y + k) % 4) * 2 + zh, d, t)
    z_peer = (y * 2 + 1 - zh, d, t)

    barrier = pltpu.get_barrier_semaphore()
    peers = [z_peer, core_peer]
    for k in (1, 2, 3):
        peers += [a_peer((zg + k) % 4), b_peer(k), x_peer(k), y_peer(k)]
    for peer in peers:
        pl.semaphore_signal(barrier, inc=1, device_id=peer, device_id_type=MESH)

    pairs = (
        (cache_h, cache_v), (enc_h, enc_v), (tok_h, tok), (ebias_h, ebias), (ret_h, ret),
        (w_h, w_v), (dbias_h, dbias), (inc_h, inc), (tgt_h, tgt),
    )
    loads = [
        pltpu.make_async_copy(src, dst, load.at[i]) for i, (src, dst) in enumerate(pairs)
    ]
    for one in loads:
        one.start()
    links = Links(send, recv)

    loads[2].wait()
    loads[3].wait()
    rows_of = lax.broadcasted_iota(jnp.int32, (256, 128), 0)
    pick = jnp.where(rows_of == tok[...], 1.0, 0.0).astype(BF16)
    bias = column_of(ebias[...], 64)
    loads[0].wait()
    loads[1].wait()
    pre = lax.dot_general(
        enc_v[...], cache_v[...], (((1,), (1,)), ((), ())), preferred_element_type=F32
    )
    every = jnp.maximum(pre + bias, 0.0).astype(BF16)
    mine = jnp.dot(every, pick, preferred_element_type=F32).astype(BF16)
    lat[x, zg, zp, c] = mine

    pl.semaphore_wait(barrier, len(peers))

    zone = (zg, zg + 1 - 2 * (zg % 2), 2 - zg // 2, 3 - 3 * (zg // 2))
    m_a = {i: links.message() for i in range(4)}
    m_b = {(k, i): links.message() for k in (1, 2, 3) for i in range(4)}
    m_x = {(k, i): links.message() for k in (1, 2, 3) for i in range(4)}
    m_c = {(k, i): links.message() for k in range(4) for i in range(4)}
    own = lat.at[x, zg, zp, c]
    for i in (3, 2, 1):
        links.start(m_a[i], own, own, a_peer(zone[i]), m_a[0] + zg)

    def spread(i):
        chunk = lat.at[x, zone[i], zp, c]
        for k in ORDER:
            links.start(m_b[k, i], chunk, chunk, b_peer(k))

    def from_far(i):
        links.arrived(m_a[0] + zone[i], lat.at[x, zone[i], zp, c], a_peer(zone[i]))
        spread(i)

    def group(k, i):
        return lat.at[(x - k + 4) % 4, zone[i], :, c]

    def to_core(k, i):
        links.start(m_c[k, i], group(k, i), group(k, i), core_peer)

    def from_group(i):
        for k in ORDER:
            links.arrived(m_b[k, i], lat.at[x, zone[i], (zp - k + 4) % 4, c], b_peer(k))
        for k in (2, 1, 3):
            links.start(m_x[k, i], group(0, i), group(0, i), x_peer(k))
        to_core(0, i)

    def from_x(i):
        for k in ORDER:
            links.arrived(m_x[k, i], group(k, i), x_peer(k))
            to_core(k, i)

    def weights(x_at, zg_at):
        first = pl.multiple_of((x_at * 4 + zg_at) * 512, 512)
        return w_v[:, pl.ds(first, 512)]

    def decode(k, i):
        x_at = (x - k + 4) % 4
        links.arrived(m_c[k, i], lat.at[x_at, zone[i], :, 1 - c], core_peer)
        block = lat[x_at, zone[i]].reshape(512, 128)
        cacc[0:168] += jnp.dot(weights(x_at, zone[i]), block, preferred_element_type=F32)

    spread(0)

    loads[4].wait()
    zero_rows = jnp.zeros((FEAT - 21, 128), F32)
    returned = jnp.concatenate([ret[...].astype(F32), zero_rows], axis=0)
    rsend[...] = jnp.concatenate([returned, jnp.zeros((8, 128), F32)], axis=0).astype(BF16)
    m_r = links.message()
    links.start(m_r, rsend, rrecv, z_peer)

    cacc[...] = jnp.zeros_like(cacc)
    for one in loads[5:]:
        one.wait()
    from_group(0)
    from_far(1)
    from_far(2)
    from_group(1)
    from_x(0)
    from_far(3)
    from_group(2)
    from_x(1)
    for k in range(4):
        decode(k, 0)
    from_group(3)
    from_x(2)
    for k in range(4):
        decode(k, 1)
    decode(0, 2)
    from_x(3)

    links.arrived(m_r, rrecv, z_peer)
    gsend[...] = jnp.concatenate([returned, rrecv[...].astype(F32)[:FEAT]], axis=0).astype(BF16)
    m_g = {k: links.message() for k in (1, 2, 3)}
    for k in ORDER:
        links.start(m_g[k], gsend, grecv.at[k - 1], y_peer(k))
    for k in ORDER:
        decode(k, 2)
    for k in range(4):
        decode(k, 3)

    def piece(offset):
        return cacc[pl.ds(offset, FEAT, stride=8), :]

    cross_of = lambda dy: (2 * dy + 1 - 2 * zh + 8) % 8
    m_y = {k: links.message() for k in (1, 2, 3)}
    for k in ORDER:
        ysend[k - 1] = jnp.concatenate([piece(2 * k), piece(cross_of(k))], axis=0).astype(BF16)
        links.start(m_y[k], ysend.at[k - 1], yrecv.at[k - 1], y_peer(k))
    base = inc[...].reshape(21, 128) + column_of(dbias[...], 21) - tgt[...].astype(F32)
    base = jnp.concatenate([base, zero_rows], axis=0)
    own_cross = piece(cross_of(0))
    e_same = base + piece(0)
    o_same = jnp.zeros((FEAT, 128), F32)
    e_cross = jnp.where(zh == 0, own_cross, 0.0)
    o_cross = jnp.where(zh == 0, 0.0, own_cross)
    for k in ORDER:
        links.arrived(m_y[k], yrecv.at[k - 1], y_peer(k))
        both = yrecv[k - 1].astype(F32)
        same, cross = both[:FEAT], both[FEAT:]
        e_same += jnp.where(y >= k, same, 0.0)
        o_same += jnp.where(y >= k, 0.0, same)
        e_cross += jnp.where(y >= k, cross, 0.0)
        o_cross += jnp.where(y >= k, 0.0, cross)
    m_z, m_o = links.message(), links.message()
    zsend[...] = jnp.concatenate([e_same, e_cross], axis=0).astype(BF16)
    links.start(m_z, zsend, zrecv, z_peer)
    osend[...] = jnp.concatenate([o_cross, jnp.zeros((8, 128), F32)], axis=0).astype(BF16)
    links.arrived(m_z, zrecv, z_peer)
    both = zrecv[...].astype(F32)
    mine_err = e_same + both[FEAT:]
    other_err = e_cross + both[:FEAT]
    esend[...] = jnp.concatenate([mine_err, other_err], axis=0).astype(BF16)
    m_e = {k: links.message() for k in (1, 2, 3)}
    for k in ORDER:
        links.start(m_e[k], esend, erecv.at[k - 1], y_peer(k))
    links.start(m_o, osend, orecv, z_peer)
    err_o[...] = mine_err[:21].astype(BF16)

    for dy in range(4):
        k = (4 - dy) % 4
        if k == 0:
            mine_b, ret_b = esend[...].astype(F32), gsend[...].astype(F32)
            same = mine_b[:FEAT]
            cross = jnp.where(zh == 0, mine_b[FEAT:], ret_b[FEAT:])
        else:
            links.arrived(m_g[k], grecv.at[k - 1], y_peer(k))
            links.arrived(m_e[k], erecv.at[k - 1], y_peer(k))
            mine_b, ret_b = erecv[k - 1].astype(F32), grecv[k - 1].astype(F32)
            both = jnp.where(y + dy < 4, mine_b, ret_b)
            same, cross = both[:FEAT], both[FEAT:]
        bk[pl.ds(2 * dy, FEAT, stride=8), :] = same
        bk[pl.ds(cross_of(dy), FEAT, stride=8), :] = cross
    back = bk[0:168].astype(BF16)

    n_c = {(k, i): links.message() for k in range(4) for i in range(4)}
    n_x = {(k, i): links.message() for k in (1, 2, 3) for i in range(4)}
    n_b = {(k, i): links.message() for k in (1, 2, 3) for i in range(4)}
    n_a = {i: links.message() for i in range(4)}

    def gradient(k, i):
        x_at = (x + k) % 4
        part = lax.dot_general(
            weights(x_at, zone[i]), back, (((0,), (0,)), ((), ())), preferred_element_type=F32
        )
        pbuf[x_at, zone[i]] = part.astype(BF16).reshape(4, 2, 64, 128)
        links.start(n_c[k, i], pbuf.at[x_at, zone[i], :, 1 - c], rc.at[k, i], core_peer)

    def chip_sum(k, i):
        links.arrived(n_c[k, i], rc.at[k, i], core_peer)
        total = pbuf[(x + k) % 4, zone[i], :, c].astype(F32) + rc[k, i].astype(F32)
        qbuf[k, i] = total.astype(BF16)
        if k > 0:
            links.start(n_x[k, i], qbuf.at[k, i], rx.at[k - 1, i], x_peer(k))

    def row_sum(i):
        total = qbuf[0, i].astype(F32)
        for k in ORDER:
            links.arrived(n_x[k, i], rx.at[k - 1, i], x_peer(k))
            total += rx[k - 1, i].astype(F32)
        ub[i] = total.astype(BF16)
        vf[i] = total
        for k in ORDER:
            links.start(n_b[k, i], ub.at[i, (zp + k) % 4], rb.at[i, k - 1], b_peer(k))

    def group_sum(i):
        total = vf[i, zp]
        for k in ORDER:
            links.arrived(n_b[k, i], rb.at[i, k - 1], b_peer(k))
            total += rb[i, k - 1].astype(F32)
        if i > 0:
            vb[i - 1] = total.astype(BF16)
            links.start(n_a[i], vb.at[i - 1], ra.at[zg], a_peer(zone[i]), n_a[0] + zg)
        return total

    steps = [(k, i) for i in (3, 2, 1, 0) for k in (2, 1, 3, 0)]
    for at, step in enumerate(steps):
        if at == 12:
            row_sum(3)
        gradient(*step)
        if at >= 2:
            chip_sum(*steps[at - 2])
    chip_sum(*steps[-2])
    chip_sum(*steps[-1])
    row_sum(2)
    group_sum(3)
    row_sum(1)
    group_sum(2)
    links.arrived(m_o, orecv, z_peer)
    outgoing = o_same + orecv[...].astype(F32)[:FEAT]
    out_o[...] = outgoing[:21].reshape(21, 1, 128)
    row_sum(0)
    group_sum(1)
    total = group_sum(0)
    for i in (3, 2, 1):
        links.arrived(n_a[0] + zone[i], ra.at[zone[i]], a_peer(zone[i]))
        total += ra[zone[i]].astype(F32)
    lg_o[...] = total
    links.drain()


def local(cache, token_ids, enc_weight, enc_bias, dec_weight, dec_bias, incoming, target, returned):
    whole = pl.BlockSpec(memory_space=pltpu.VMEM)
    left = pl.BlockSpec(memory_space=pltpu.HBM)
    weights = jnp.transpose(dec_weight[0], (1, 0, 2)).reshape(168, 8192)
    err, out, grad = pl.pallas_call(
        kernel,
        out_shape=(
            jax.ShapeDtypeStruct((21, 128), BF16),
            jax.ShapeDtypeStruct((21, 1, 128), F32),
            jax.ShapeDtypeStruct((64, 128), F32),
        ),
        in_specs=[left] * 9,
        out_specs=(whole, whole, whole),
        scratch_shapes=[
            pltpu.VMEM((1, 128), jnp.int32),
            pltpu.VMEM((1, 64), F32),
            pltpu.VMEM((1, 21), F32),
            pltpu.VMEM((21, 1, 128), F32),
            pltpu.VMEM((21, 128), BF16),
            pltpu.VMEM((21, 128), BF16),
            pltpu.VMEM((256, 5376), BF16),
            pltpu.VMEM((64, 5376), BF16),
            pltpu.VMEM((168, 8192), BF16),
            pltpu.VMEM((4, 4, 4, 2, 64, 128), BF16),
            pltpu.VMEM((4, 4, 4, 2, 64, 128), BF16),
            pltpu.VMEM((4, 4, 4, 64, 128), BF16),
            pltpu.VMEM((4, 4, 4, 64, 128), BF16),
            pltpu.VMEM((3, 4, 4, 64, 128), BF16),
            pltpu.VMEM((4, 4, 64, 128), BF16),
            pltpu.VMEM((4, 3, 64, 128), BF16),
            pltpu.VMEM((4, 4, 64, 128), F32),
            pltpu.VMEM((3, 64, 128), BF16),
            pltpu.VMEM((4, 64, 128), BF16),
            pltpu.VMEM((192, 128), F32),
            pltpu.VMEM((192, 128), F32),
            pltpu.VMEM((3, 48, 128), BF16),
            pltpu.VMEM((3, 48, 128), BF16),
            pltpu.VMEM((48, 128), BF16),
            pltpu.VMEM((48, 128), BF16),
            pltpu.VMEM((32, 128), BF16),
            pltpu.VMEM((32, 128), BF16),
            pltpu.VMEM((48, 128), BF16),
            pltpu.VMEM((3, 48, 128), BF16),
            pltpu.VMEM((32, 128), BF16),
            pltpu.VMEM((32, 128), BF16),
            pltpu.VMEM((48, 128), BF16),
            pltpu.VMEM((3, 48, 128), BF16),
            pltpu.SemaphoreType.DMA((9,)),
            pltpu.SemaphoreType.DMA((MESSAGES,)),
            pltpu.SemaphoreType.DMA((MESSAGES,)),
        ],
        compiler_params=pltpu.CompilerParams(
            collective_id=0, has_side_effects=True, vmem_limit_bytes=64 << 20
        ),
        name="transcoder",
    )(
        token_ids.reshape(1, 128),
        enc_bias,
        dec_bias,
        jnp.transpose(incoming, (2, 0, 1)),
        target[0].T,
        returned[0].T,
        cache[0],
        enc_weight[0],
        weights,
    )
    return (err.T[None], jnp.transpose(out, (1, 2, 0)), grad[None])


def solution(mesh):
    placed = (
        P("section", None, None),
        P(),
        P("section", ("dp", "tensor"), None),
        P("section", ("dp", "tensor")),
        P("section", None, ("dp", "tensor"), None),
        P("section", ("dp", "tensor")),
        P("section", None, ("dp", "tensor")),
        P("section", None, ("dp", "tensor")),
        P("section", None, ("dp", "tensor")),
    )
    return jax.shard_map(
        local,
        mesh=mesh,
        in_specs=placed,
        out_specs=(
            P("section", None, ("dp", "tensor")),
            P("section", None, ("dp", "tensor")),
            P("section", ("dp", "tensor"), None),
        ),
        check_vma=False,
    )
```

```python
import jax
import jax.numpy as jnp
from jax import lax
from jax.experimental import pallas as pl
from jax.experimental.pallas import tpu as pltpu
from jax.sharding import PartitionSpec as P

MESH = pl.DeviceIdType.MESH
F32 = jnp.float32
BF16 = jnp.bfloat16
FEAT = 24
ORDER = (1, 3, 2)


class Links:
    def __init__(self, send, recv):
        self.send, self.recv, self.used, self.open = send, recv, 0, []

    def message(self):
        self.used += 1
        return self.used - 1

    def copy(self, index, src, dst, peer, lands=None):
        return pltpu.make_async_remote_copy(
            src_ref=src,
            dst_ref=dst,
            send_sem=self.send.at[index],
            recv_sem=self.recv.at[index if lands is None else lands],
            device_id=peer,
            device_id_type=MESH,
        )

    def start(self, index, src, dst, peer, lands=None):
        copy = self.copy(index, src, dst, peer, lands)
        copy.start()
        self.open.append(copy)

    def arrived(self, index, dst, peer):
        self.copy(index, dst, dst, peer).wait_recv()

    def drain(self):
        for copy in self.open:
            copy.wait_send()


MESSAGES = 112
LAG = 9


def column_of(row, rows):
    n = row.shape[1]
    down = lax.broadcasted_iota(jnp.int32, (rows, n), 0)
    along = lax.broadcasted_iota(jnp.int32, (rows, n), 1)
    return jnp.sum(jnp.where(down == along, row, 0.0), axis=1, keepdims=True)


def kernel(
    tok_h, ebias_h, dbias_h, inc_h, tgt_h, ret_h, cache_h, enc_h, w_h,
    err_o, out_o, lg_o, tok, ebias, dbias, inc, tgt, ret,
    cache_v, enc_v, w_v, lat, pbuf, rc, qbuf, rx, ub, rb, vf, vb, ra,
    cacc, bk, ysend, yrecv, zsend, zrecv, osend, orecv, esend, erecv,
    rsend, rrecv, gsend, grecv, load, send, recv,
):
    s, d, t = lax.axis_index("section"), lax.axis_index("dp"), lax.axis_index("tensor")
    y, zh, x, z, c = s // 2, s % 2, d, t // 2, t % 2
    zg, zp = z // 4, z % 4
    core_peer = (s, d, z * 2 + 1 - c)
    x_peer = lambda k: (s, (x + k) % 4, t)
    a_peer = lambda at: (s, d, (at * 4 + zp) * 2 + c)
    b_peer = lambda k: (s, d, (zg * 4 + (zp + k) % 4) * 2 + c)
    y_peer = lambda k: (((y + k) % 4) * 2 + zh, d, t)
    z_peer = (y * 2 + 1 - zh, d, t)

    barrier = pltpu.get_barrier_semaphore()
    peers = [z_peer, core_peer]
    for k in (1, 2, 3):
        peers += [a_peer((zg + k) % 4), b_peer(k), x_peer(k), y_peer(k)]
    for peer in peers:
        pl.semaphore_signal(barrier, inc=1, device_id=peer, device_id_type=MESH)

    pairs = (
        (cache_h, cache_v), (enc_h, enc_v), (tok_h, tok), (ebias_h, ebias), (ret_h, ret),
        (w_h, w_v), (dbias_h, dbias), (inc_h, inc), (tgt_h, tgt),
    )
    loads = [
        pltpu.make_async_copy(src, dst, load.at[i]) for i, (src, dst) in enumerate(pairs)
    ]
    for one in loads:
        one.start()
    links = Links(send, recv)

    loads[2].wait()
    loads[3].wait()
    rows_of = lax.broadcasted_iota(jnp.int32, (256, 128), 0)
    pick = jnp.where(rows_of == tok[...], 1.0, 0.0).astype(BF16)
    bias = column_of(ebias[...], 64)
    loads[0].wait()
    loads[1].wait()
    pre = lax.dot_general(
        enc_v[...], cache_v[...], (((1,), (1,)), ((), ())), preferred_element_type=F32
    )
    every = jnp.maximum(pre + bias, 0.0).astype(BF16)
    mine = jnp.dot(every, pick, preferred_element_type=F32).astype(BF16)
    lat[x, zg, zp, c] = mine

    pl.semaphore_wait(barrier, len(peers))

    zone = (zg, zg + 1 - 2 * (zg % 2), 2 - zg // 2, 3 - 3 * (zg // 2))
    m_a = {i: links.message() for i in range(4)}
    m_b = {(k, i): links.message() for k in (1, 2, 3) for i in range(4)}
    m_x = {(k, i): links.message() for k in (1, 2, 3) for i in range(4)}
    m_c = {(k, i): links.message() for k in range(4) for i in range(4)}
    own = lat.at[x, zg, zp, c]
    for i in (3, 2, 1):
        links.start(m_a[i], own, own, a_peer(zone[i]), m_a[0] + zg)

    def spread(i):
        chunk = lat.at[x, zone[i], zp, c]
        for k in ORDER:
            links.start(m_b[k, i], chunk, chunk, b_peer(k))

    def from_far(i):
        links.arrived(m_a[0] + zone[i], lat.at[x, zone[i], zp, c], a_peer(zone[i]))
        spread(i)

    def group(k, i):
        return lat.at[(x - k + 4) % 4, zone[i], :, c]

    def to_core(k, i):
        links.start(m_c[k, i], group(k, i), group(k, i), core_peer)

    def from_group(i):
        for k in ORDER:
            links.arrived(m_b[k, i], lat.at[x, zone[i], (zp - k + 4) % 4, c], b_peer(k))
        for k in (2, 1, 3):
            links.start(m_x[k, i], group(0, i), group(0, i), x_peer(k))
        to_core(0, i)

    def from_x(i):
        for k in ORDER:
            links.arrived(m_x[k, i], group(k, i), x_peer(k))
            to_core(k, i)

    def weights(x_at, zg_at):
        first = pl.multiple_of((x_at * 4 + zg_at) * 512, 512)
        return w_v[:, pl.ds(first, 512)]

    def decode(k, i):
        x_at = (x - k + 4) % 4
        links.arrived(m_c[k, i], lat.at[x_at, zone[i], :, 1 - c], core_peer)
        block = lat[x_at, zone[i]].reshape(512, 128)
        cacc[0:168] += jnp.dot(weights(x_at, zone[i]), block, preferred_element_type=F32)

    spread(0)

    cacc[...] = jnp.zeros_like(cacc)
    for one in loads[4:]:
        one.wait()
    from_group(0)
    from_far(1)
    from_far(2)
    from_group(1)
    from_x(0)
    from_far(3)
    from_group(2)
    from_x(1)
    for k in range(4):
        decode(k, 0)
    from_group(3)

    zero_rows = jnp.zeros((FEAT - 21, 128), F32)
    returned = jnp.concatenate([ret[...].astype(F32), zero_rows], axis=0)
    rsend[...] = jnp.concatenate([returned, jnp.zeros((8, 128), F32)], axis=0).astype(BF16)
    m_r = links.message()
    links.start(m_r, rsend, rrecv, z_peer)

    from_x(2)
    for k in range(4):
        decode(k, 1)
    decode(0, 2)
    from_x(3)

    for k in ORDER:
        decode(k, 2)
    for k in range(4):
        decode(k, 3)

    def piece(offset):
        return cacc[pl.ds(offset, FEAT, stride=8), :]

    cross_of = lambda dy: (2 * dy + 1 - 2 * zh + 8) % 8
    m_y = {k: links.message() for k in (1, 2, 3)}
    for k in ORDER:
        ysend[k - 1] = jnp.concatenate([piece(2 * k), piece(cross_of(k))], axis=0).astype(BF16)
        links.start(m_y[k], ysend.at[k - 1], yrecv.at[k - 1], y_peer(k))
    base = inc[...].reshape(21, 128) + column_of(dbias[...], 21) - tgt[...].astype(F32)
    base = jnp.concatenate([base, zero_rows], axis=0)
    own_cross = piece(cross_of(0))
    e_same = base + piece(0)
    o_same = jnp.zeros((FEAT, 128), F32)
    e_cross = jnp.where(zh == 0, own_cross, 0.0)
    o_cross = jnp.where(zh == 0, 0.0, own_cross)
    for k in ORDER:
        links.arrived(m_y[k], yrecv.at[k - 1], y_peer(k))
        both = yrecv[k - 1].astype(F32)
        same, cross = both[:FEAT], both[FEAT:]
        e_same += jnp.where(y >= k, same, 0.0)
        o_same += jnp.where(y >= k, 0.0, same)
        e_cross += jnp.where(y >= k, cross, 0.0)
        o_cross += jnp.where(y >= k, 0.0, cross)
    m_z, m_o = links.message(), links.message()
    zsend[...] = jnp.concatenate([e_same, e_cross], axis=0).astype(BF16)
    links.start(m_z, zsend, zrecv, z_peer)
    osend[...] = jnp.concatenate([o_cross, jnp.zeros((8, 128), F32)], axis=0).astype(BF16)

    links.arrived(m_r, rrecv, z_peer)
    gsend[...] = jnp.concatenate([returned, rrecv[...].astype(F32)[:FEAT]], axis=0).astype(BF16)
    m_g = {k: links.message() for k in (1, 2, 3)}
    for k in ORDER:
        links.start(m_g[k], gsend, grecv.at[k - 1], y_peer(k))

    links.arrived(m_z, zrecv, z_peer)
    both = zrecv[...].astype(F32)
    mine_err = e_same + both[FEAT:]
    other_err = e_cross + both[:FEAT]
    esend[...] = jnp.concatenate([mine_err, other_err], axis=0).astype(BF16)
    m_e = {k: links.message() for k in (1, 2, 3)}
    for k in ORDER:
        links.start(m_e[k], esend, erecv.at[k - 1], y_peer(k))
    links.start(m_o, osend, orecv, z_peer)
    err_o[...] = mine_err[:21].astype(BF16)

    for dy in range(4):
        k = (4 - dy) % 4
        if k == 0:
            mine_b, ret_b = esend[...].astype(F32), gsend[...].astype(F32)
            same = mine_b[:FEAT]
            cross = jnp.where(zh == 0, mine_b[FEAT:], ret_b[FEAT:])
        else:
            links.arrived(m_g[k], grecv.at[k - 1], y_peer(k))
            links.arrived(m_e[k], erecv.at[k - 1], y_peer(k))
            mine_b, ret_b = erecv[k - 1].astype(F32), grecv[k - 1].astype(F32)
            both = jnp.where(y + dy < 4, mine_b, ret_b)
            same, cross = both[:FEAT], both[FEAT:]
        bk[pl.ds(2 * dy, FEAT, stride=8), :] = same
        bk[pl.ds(cross_of(dy), FEAT, stride=8), :] = cross
    back = bk[0:168].astype(BF16)

    n_c = {(k, i): links.message() for k in range(4) for i in range(4)}
    n_x = {(k, i): links.message() for k in (1, 2, 3) for i in range(4)}
    n_b = {(k, i): links.message() for k in (1, 2, 3) for i in range(4)}
    n_a = {i: links.message() for i in range(4)}

    def gradient(k, i):
        x_at = (x + k) % 4
        part = lax.dot_general(
            weights(x_at, zone[i]), back, (((0,), (0,)), ((), ())), preferred_element_type=F32
        )
        pbuf[x_at, zone[i]] = part.astype(BF16).reshape(4, 2, 64, 128)
        links.start(n_c[k, i], pbuf.at[x_at, zone[i], :, 1 - c], rc.at[k, i], core_peer)

    def chip_sum(k, i):
        links.arrived(n_c[k, i], rc.at[k, i], core_peer)
        total = pbuf[(x + k) % 4, zone[i], :, c].astype(F32) + rc[k, i].astype(F32)
        qbuf[k, i] = total.astype(BF16)
        if k > 0:
            links.start(n_x[k, i], qbuf.at[k, i], rx.at[k - 1, i], x_peer(k))

    def row_sum(i):
        total = qbuf[0, i].astype(F32)
        for k in ORDER:
            links.arrived(n_x[k, i], rx.at[k - 1, i], x_peer(k))
            total += rx[k - 1, i].astype(F32)
        ub[i] = total.astype(BF16)
        vf[i] = total
        for k in ORDER:
            links.start(n_b[k, i], ub.at[i, (zp + k) % 4], rb.at[i, k - 1], b_peer(k))

    def group_sum(i):
        total = vf[i, zp]
        for k in ORDER:
            links.arrived(n_b[k, i], rb.at[i, k - 1], b_peer(k))
            total += rb[i, k - 1].astype(F32)
        if i > 0:
            vb[i - 1] = total.astype(BF16)
            links.start(n_a[i], vb.at[i - 1], ra.at[zg], a_peer(zone[i]), n_a[0] + zg)
        return total

    steps = [(k, i) for i in (3, 2, 1, 0) for k in (2, 1, 3, 0)]
    for at in range(len(steps) + LAG):
        if at < len(steps):
            gradient(*steps[at])
        if at >= LAG:
            chip_sum(*steps[at - LAG])
    row_sum(3)
    row_sum(2)
    group_sum(3)
    row_sum(1)
    group_sum(2)
    links.arrived(m_o, orecv, z_peer)
    outgoing = o_same + orecv[...].astype(F32)[:FEAT]
    out_o[...] = outgoing[:21].reshape(21, 1, 128)
    row_sum(0)
    group_sum(1)
    total = group_sum(0)
    for i in (3, 2, 1):
        links.arrived(n_a[0] + zone[i], ra.at[zone[i]], a_peer(zone[i]))
        total += ra[zone[i]].astype(F32)
    lg_o[...] = total
    links.drain()


def hand_over(*refs):
    moves = [pltpu.make_async_copy(refs[i], refs[i + 3], refs[6].at[i]) for i in range(3)]
    for move in moves:
        move.start()
    for move in moves:
        move.wait()


def local(cache, token_ids, enc_weight, enc_bias, dec_weight, dec_bias, incoming, target, returned):
    whole = pl.BlockSpec(memory_space=pltpu.VMEM)
    left = pl.BlockSpec(memory_space=pltpu.HBM)
    weights = jnp.transpose(dec_weight[0], (1, 0, 2)).reshape(168, 8192)
    shapes = (
        jax.ShapeDtypeStruct((21, 128), BF16),
        jax.ShapeDtypeStruct((21, 1, 128), F32),
        jax.ShapeDtypeStruct((64, 128), F32),
    )
    results = pl.pallas_call(
        kernel,
        out_shape=shapes,
        in_specs=[left] * 9,
        out_specs=(whole, whole, whole),
        scratch_shapes=[
            pltpu.VMEM((1, 128), jnp.int32),
            pltpu.VMEM((1, 64), F32),
            pltpu.VMEM((1, 21), F32),
            pltpu.VMEM((21, 1, 128), F32),
            pltpu.VMEM((21, 128), BF16),
            pltpu.VMEM((21, 128), BF16),
            pltpu.VMEM((256, 5376), BF16),
            pltpu.VMEM((64, 5376), BF16),
            pltpu.VMEM((168, 8192), BF16),
            pltpu.VMEM((4, 4, 4, 2, 64, 128), BF16),
            pltpu.VMEM((4, 4, 4, 2, 64, 128), BF16),
            pltpu.VMEM((4, 4, 4, 64, 128), BF16),
            pltpu.VMEM((4, 4, 4, 64, 128), BF16),
            pltpu.VMEM((3, 4, 4, 64, 128), BF16),
            pltpu.VMEM((4, 4, 64, 128), BF16),
            pltpu.VMEM((4, 3, 64, 128), BF16),
            pltpu.VMEM((4, 4, 64, 128), F32),
            pltpu.VMEM((3, 64, 128), BF16),
            pltpu.VMEM((4, 64, 128), BF16),
            pltpu.VMEM((192, 128), F32),
            pltpu.VMEM((192, 128), F32),
            pltpu.VMEM((3, 48, 128), BF16),
            pltpu.VMEM((3, 48, 128), BF16),
            pltpu.VMEM((48, 128), BF16),
            pltpu.VMEM((48, 128), BF16),
            pltpu.VMEM((32, 128), BF16),
            pltpu.VMEM((32, 128), BF16),
            pltpu.VMEM((48, 128), BF16),
            pltpu.VMEM((3, 48, 128), BF16),
            pltpu.VMEM((32, 128), BF16),
            pltpu.VMEM((32, 128), BF16),
            pltpu.VMEM((48, 128), BF16),
            pltpu.VMEM((3, 48, 128), BF16),
            pltpu.SemaphoreType.DMA((9,)),
            pltpu.SemaphoreType.DMA((MESSAGES,)),
            pltpu.SemaphoreType.DMA((MESSAGES,)),
        ],
        compiler_params=pltpu.CompilerParams(
            collective_id=0, has_side_effects=True, vmem_limit_bytes=64 << 20
        ),
        name="transcoder",
    )(
        token_ids.reshape(1, 128),
        enc_bias,
        dec_bias,
        jnp.transpose(incoming, (2, 0, 1)),
        target[0].T,
        returned[0].T,
        cache[0],
        enc_weight[0],
        weights,
    )
    err, out, grad = pl.pallas_call(
        hand_over,
        out_shape=shapes,
        in_specs=[left] * 3,
        out_specs=(left, left, left),
        scratch_shapes=[pltpu.SemaphoreType.DMA((3,))],
        compiler_params=pltpu.CompilerParams(vmem_limit_bytes=64 << 20),
        name="results",
    )(*results)
    return (err.T[None], jnp.transpose(out, (1, 2, 0)), grad[None])


def solution(mesh):
    placed = (
        P("section", None, None),
        P(),
        P("section", ("dp", "tensor"), None),
        P("section", ("dp", "tensor")),
        P("section", None, ("dp", "tensor"), None),
        P("section", ("dp", "tensor")),
        P("section", None, ("dp", "tensor")),
        P("section", None, ("dp", "tensor")),
        P("section", None, ("dp", "tensor")),
    )
    return jax.shard_map(
        local,
        mesh=mesh,
        in_specs=placed,
        out_specs=(
            P("section", None, ("dp", "tensor")),
            P("section", None, ("dp", "tensor")),
            P("section", ("dp", "tensor"), None),
        ),
        check_vma=False,
    )
```

```python
import jax
import jax.numpy as jnp
from jax import lax
from jax.experimental import pallas as pl
from jax.experimental.pallas import tpu as pltpu
from jax.sharding import PartitionSpec as P

MESH = pl.DeviceIdType.MESH
F32 = jnp.float32
BF16 = jnp.bfloat16
FEAT = 24
ORDER = (1, 3, 2)


class Links:
    def __init__(self, send, recv):
        self.send, self.recv, self.used, self.open = send, recv, 0, []

    def message(self):
        self.used += 1
        return self.used - 1

    def copy(self, index, src, dst, peer, lands=None):
        return pltpu.make_async_remote_copy(
            src_ref=src,
            dst_ref=dst,
            send_sem=self.send.at[index],
            recv_sem=self.recv.at[index if lands is None else lands],
            device_id=peer,
            device_id_type=MESH,
        )

    def start(self, index, src, dst, peer, lands=None):
        copy = self.copy(index, src, dst, peer, lands)
        copy.start()
        self.open.append(copy)

    def arrived(self, index, dst, peer):
        self.copy(index, dst, dst, peer).wait_recv()

    def drain(self):
        for copy in self.open:
            copy.wait_send()


MESSAGES = 112
LAG = 9


def column_of(row, rows):
    n = row.shape[1]
    down = lax.broadcasted_iota(jnp.int32, (rows, n), 0)
    along = lax.broadcasted_iota(jnp.int32, (rows, n), 1)
    return jnp.sum(jnp.where(down == along, row, 0.0), axis=1, keepdims=True)


def kernel(
    tok_h, ebias_h, dbias_h, inc_h, tgt_h, ret_h, cache_h, enc_h, w_h,
    err_o, out_o, lg_o, tok, ebias, dbias, inc, tgt, ret,
    cache_v, enc_v, w_v, lat, pbuf, rc, qbuf, rx, ub, rb, vf, vb, ra,
    cacc, bk, ysend, yrecv, zsend, zrecv, osend, orecv, esend, erecv,
    rsend, rrecv, gsend, grecv, load, send, recv,
):
    s, d, t = lax.axis_index("section"), lax.axis_index("dp"), lax.axis_index("tensor")
    y, zh, x, z, c = s // 2, s % 2, d, t // 2, t % 2
    zg, zp = z // 4, z % 4
    core_peer = (s, d, z * 2 + 1 - c)
    x_peer = lambda k: (s, (x + k) % 4, t)
    a_peer = lambda at: (s, d, (at * 4 + zp) * 2 + c)
    b_peer = lambda k: (s, d, (zg * 4 + (zp + k) % 4) * 2 + c)
    y_peer = lambda k: (((y + k) % 4) * 2 + zh, d, t)
    z_peer = (y * 2 + 1 - zh, d, t)

    barrier = pltpu.get_barrier_semaphore()
    peers = [z_peer, core_peer]
    for k in (1, 2, 3):
        peers += [a_peer((zg + k) % 4), b_peer(k), x_peer(k), y_peer(k)]
    for peer in peers:
        pl.semaphore_signal(barrier, inc=1, device_id=peer, device_id_type=MESH)

    pairs = (
        (cache_h, cache_v), (enc_h, enc_v), (tok_h, tok), (ebias_h, ebias), (ret_h, ret),
        (w_h, w_v), (dbias_h, dbias), (inc_h, inc), (tgt_h, tgt),
    )
    loads = [
        pltpu.make_async_copy(src, dst, load.at[i]) for i, (src, dst) in enumerate(pairs)
    ]
    for one in loads:
        one.start()
    links = Links(send, recv)

    loads[2].wait()
    loads[3].wait()
    rows_of = lax.broadcasted_iota(jnp.int32, (256, 128), 0)
    pick = jnp.where(rows_of == tok[...], 1.0, 0.0).astype(BF16)
    bias = column_of(ebias[...], 64)
    loads[0].wait()
    loads[1].wait()
    pre = lax.dot_general(
        enc_v[...], cache_v[...], (((1,), (1,)), ((), ())), preferred_element_type=F32
    )
    every = jnp.maximum(pre + bias, 0.0).astype(BF16)
    mine = jnp.dot(every, pick, preferred_element_type=F32).astype(BF16)
    lat[x, zg, zp, c] = mine

    pl.semaphore_wait(barrier, len(peers))

    zone = (zg, zg + 1 - 2 * (zg % 2), 2 - zg // 2, 3 - 3 * (zg // 2))
    m_a = {i: links.message() for i in range(4)}
    m_b = {(k, i): links.message() for k in (1, 2, 3) for i in range(4)}
    m_x = {(k, i): links.message() for k in (1, 2, 3) for i in range(4)}
    m_c = {(k, i): links.message() for k in range(4) for i in range(4)}
    own = lat.at[x, zg, zp, c]
    for i in (3, 2, 1):
        links.start(m_a[i], own, own, a_peer(zone[i]), m_a[0] + zg)

    def spread(i):
        chunk = lat.at[x, zone[i], zp, c]
        for k in ORDER:
            links.start(m_b[k, i], chunk, chunk, b_peer(k))

    def from_far(i):
        links.arrived(m_a[0] + zone[i], lat.at[x, zone[i], zp, c], a_peer(zone[i]))
        spread(i)

    def group(k, i):
        return lat.at[(x - k + 4) % 4, zone[i], :, c]

    def to_core(k, i):
        links.start(m_c[k, i], group(k, i), group(k, i), core_peer)

    def from_group(i):
        for k in ORDER:
            links.arrived(m_b[k, i], lat.at[x, zone[i], (zp - k + 4) % 4, c], b_peer(k))
        for k in (2, 1, 3):
            links.start(m_x[k, i], group(0, i), group(0, i), x_peer(k))
        to_core(0, i)

    def from_x(i):
        for k in ORDER:
            links.arrived(m_x[k, i], group(k, i), x_peer(k))
            to_core(k, i)

    def weights(x_at, zg_at):
        first = pl.multiple_of((x_at * 4 + zg_at) * 512, 512)
        return w_v[:, pl.ds(first, 512)]

    def decode(k, i):
        x_at = (x - k + 4) % 4
        links.arrived(m_c[k, i], lat.at[x_at, zone[i], :, 1 - c], core_peer)
        block = lat[x_at, zone[i]].reshape(512, 128)
        cacc[0:168] += jnp.dot(weights(x_at, zone[i]), block, preferred_element_type=F32)

    spread(0)

    cacc[...] = jnp.zeros_like(cacc)
    for one in loads[4:]:
        one.wait()
    from_group(0)
    from_far(1)
    from_far(2)
    from_group(1)
    from_x(0)
    from_far(3)
    from_group(2)
    from_x(1)
    for k in range(4):
        decode(k, 0)
    from_group(3)

    zero_rows = jnp.zeros((FEAT - 21, 128), F32)
    returned = jnp.concatenate([ret[...].astype(F32), zero_rows], axis=0)
    rsend[...] = jnp.concatenate([returned, jnp.zeros((8, 128), F32)], axis=0).astype(BF16)
    m_r = links.message()
    links.start(m_r, rsend, rrecv, z_peer)

    from_x(2)
    for k in range(4):
        decode(k, 1)
    decode(0, 2)
    from_x(3)

    for k in ORDER:
        decode(k, 2)
    for k in range(4):
        decode(k, 3)

    def piece(offset):
        return cacc[pl.ds(offset, FEAT, stride=8), :]

    cross_of = lambda dy: (2 * dy + 1 - 2 * zh + 8) % 8
    m_y = {k: links.message() for k in (1, 2, 3)}
    for k in ORDER:
        ysend[k - 1] = jnp.concatenate([piece(2 * k), piece(cross_of(k))], axis=0).astype(BF16)
        links.start(m_y[k], ysend.at[k - 1], yrecv.at[k - 1], y_peer(k))
    base = inc[...].reshape(21, 128) + column_of(dbias[...], 21) - tgt[...].astype(F32)
    base = jnp.concatenate([base, zero_rows], axis=0)
    own_cross = piece(cross_of(0))
    e_same = base + piece(0)
    o_same = jnp.zeros((FEAT, 128), F32)
    e_cross = jnp.where(zh == 0, own_cross, 0.0)
    o_cross = jnp.where(zh == 0, 0.0, own_cross)
    for k in ORDER:
        links.arrived(m_y[k], yrecv.at[k - 1], y_peer(k))
        both = yrecv[k - 1].astype(F32)
        same, cross = both[:FEAT], both[FEAT:]
        e_same += jnp.where(y >= k, same, 0.0)
        o_same += jnp.where(y >= k, 0.0, same)
        e_cross += jnp.where(y >= k, cross, 0.0)
        o_cross += jnp.where(y >= k, 0.0, cross)
    m_z, m_o = links.message(), links.message()
    zsend[...] = jnp.concatenate([e_same, e_cross], axis=0).astype(BF16)
    links.start(m_z, zsend, zrecv, z_peer)
    osend[...] = jnp.concatenate([o_cross, jnp.zeros((8, 128), F32)], axis=0).astype(BF16)

    links.arrived(m_r, rrecv, z_peer)
    gsend[...] = jnp.concatenate([returned, rrecv[...].astype(F32)[:FEAT]], axis=0).astype(BF16)
    m_g = {k: links.message() for k in (1, 2, 3)}
    for k in ORDER:
        links.start(m_g[k], gsend, grecv.at[k - 1], y_peer(k))

    links.arrived(m_z, zrecv, z_peer)
    both = zrecv[...].astype(F32)
    mine_err = e_same + both[FEAT:]
    other_err = e_cross + both[:FEAT]
    esend[...] = jnp.concatenate([mine_err, other_err], axis=0).astype(BF16)
    m_e = {k: links.message() for k in (1, 2, 3)}
    for k in ORDER:
        links.start(m_e[k], esend, erecv.at[k - 1], y_peer(k))
    links.start(m_o, osend, orecv, z_peer)
    err_o[...] = mine_err[:21].astype(BF16)

    for dy in range(4):
        k = (4 - dy) % 4
        if k == 0:
            mine_b, ret_b = esend[...].astype(F32), gsend[...].astype(F32)
            same = mine_b[:FEAT]
            cross = jnp.where(zh == 0, mine_b[FEAT:], ret_b[FEAT:])
        else:
            links.arrived(m_g[k], grecv.at[k - 1], y_peer(k))
            links.arrived(m_e[k], erecv.at[k - 1], y_peer(k))
            mine_b, ret_b = erecv[k - 1].astype(F32), grecv[k - 1].astype(F32)
            both = jnp.where(y + dy < 4, mine_b, ret_b)
            same, cross = both[:FEAT], both[FEAT:]
        bk[pl.ds(2 * dy, FEAT, stride=8), :] = same
        bk[pl.ds(cross_of(dy), FEAT, stride=8), :] = cross
    back = bk[0:168].astype(BF16)

    n_c = {(k, i): links.message() for k in range(4) for i in range(4)}
    n_x = {(k, i): links.message() for k in (1, 2, 3) for i in range(4)}
    n_b = {(k, i): links.message() for k in (1, 2, 3) for i in range(4)}
    n_a = {i: links.message() for i in range(4)}

    def gradient(k, i):
        x_at = (x + k) % 4
        part = lax.dot_general(
            weights(x_at, zone[i]), back, (((0,), (0,)), ((), ())), preferred_element_type=F32
        )
        pbuf[x_at, zone[i]] = part.astype(BF16).reshape(4, 2, 64, 128)
        links.start(n_c[k, i], pbuf.at[x_at, zone[i], :, 1 - c], rc.at[k, i], core_peer)

    def chip_sum(k, i):
        links.arrived(n_c[k, i], rc.at[k, i], core_peer)
        total = pbuf[(x + k) % 4, zone[i], :, c].astype(F32) + rc[k, i].astype(F32)
        qbuf[k, i] = total.astype(BF16)
        if k > 0:
            links.start(n_x[k, i], qbuf.at[k, i], rx.at[k - 1, i], x_peer(k))

    def row_sum(i):
        total = qbuf[0, i].astype(F32)
        for k in ORDER:
            links.arrived(n_x[k, i], rx.at[k - 1, i], x_peer(k))
            total += rx[k - 1, i].astype(F32)
        ub[i] = total.astype(BF16)
        vf[i] = total
        for k in ORDER:
            links.start(n_b[k, i], ub.at[i, (zp + k) % 4], rb.at[i, k - 1], b_peer(k))

    def group_sum(i):
        total = vf[i, zp]
        for k in ORDER:
            links.arrived(n_b[k, i], rb.at[i, k - 1], b_peer(k))
            total += rb[i, k - 1].astype(F32)
        if i > 0:
            vb[i - 1] = total.astype(BF16)
            links.start(n_a[i], vb.at[i - 1], ra.at[zg], a_peer(zone[i]), n_a[0] + zg)
        return total

    steps = [(k, i) for i in (3, 2, 1, 0) for k in (2, 1, 3, 0)]
    for at in range(len(steps) + LAG):
        if at < len(steps):
            gradient(*steps[at])
        if at >= LAG:
            chip_sum(*steps[at - LAG])
        if at == 11 + LAG:
            row_sum(3)
    row_sum(2)
    group_sum(3)
    row_sum(1)
    group_sum(2)
    links.arrived(m_o, orecv, z_peer)
    outgoing = o_same + orecv[...].astype(F32)[:FEAT]
    out_o[...] = outgoing[:21].reshape(21, 1, 128)
    row_sum(0)
    group_sum(1)
    total = group_sum(0)
    for i in (3, 2, 1):
        links.arrived(n_a[0] + zone[i], ra.at[zone[i]], a_peer(zone[i]))
        total += ra[zone[i]].astype(F32)
    lg_o[...] = total
    links.drain()


def hand_over(*refs):
    moves = [pltpu.make_async_copy(refs[i], refs[i + 3], refs[6].at[i]) for i in range(3)]
    for move in moves:
        move.start()
    for move in moves:
        move.wait()


def local(cache, token_ids, enc_weight, enc_bias, dec_weight, dec_bias, incoming, target, returned):
    whole = pl.BlockSpec(memory_space=pltpu.VMEM)
    left = pl.BlockSpec(memory_space=pltpu.HBM)
    weights = jnp.transpose(dec_weight[0], (1, 0, 2)).reshape(168, 8192)
    shapes = (
        jax.ShapeDtypeStruct((21, 128), BF16),
        jax.ShapeDtypeStruct((21, 1, 128), F32),
        jax.ShapeDtypeStruct((64, 128), F32),
    )
    results = pl.pallas_call(
        kernel,
        out_shape=shapes,
        in_specs=[left] * 9,
        out_specs=(whole, whole, whole),
        scratch_shapes=[
            pltpu.VMEM((1, 128), jnp.int32),
            pltpu.VMEM((1, 64), F32),
            pltpu.VMEM((1, 21), F32),
            pltpu.VMEM((21, 1, 128), F32),
            pltpu.VMEM((21, 128), BF16),
            pltpu.VMEM((21, 128), BF16),
            pltpu.VMEM((256, 5376), BF16),
            pltpu.VMEM((64, 5376), BF16),
            pltpu.VMEM((168, 8192), BF16),
            pltpu.VMEM((4, 4, 4, 2, 64, 128), BF16),
            pltpu.VMEM((4, 4, 4, 2, 64, 128), BF16),
            pltpu.VMEM((4, 4, 4, 64, 128), BF16),
            pltpu.VMEM((4, 4, 4, 64, 128), BF16),
            pltpu.VMEM((3, 4, 4, 64, 128), BF16),
            pltpu.VMEM((4, 4, 64, 128), BF16),
            pltpu.VMEM((4, 3, 64, 128), BF16),
            pltpu.VMEM((4, 4, 64, 128), F32),
            pltpu.VMEM((3, 64, 128), BF16),
            pltpu.VMEM((4, 64, 128), BF16),
            pltpu.VMEM((192, 128), F32),
            pltpu.VMEM((192, 128), F32),
            pltpu.VMEM((3, 48, 128), BF16),
            pltpu.VMEM((3, 48, 128), BF16),
            pltpu.VMEM((48, 128), BF16),
            pltpu.VMEM((48, 128), BF16),
            pltpu.VMEM((32, 128), BF16),
            pltpu.VMEM((32, 128), BF16),
            pltpu.VMEM((48, 128), BF16),
            pltpu.VMEM((3, 48, 128), BF16),
            pltpu.VMEM((32, 128), BF16),
            pltpu.VMEM((32, 128), BF16),
            pltpu.VMEM((48, 128), BF16),
            pltpu.VMEM((3, 48, 128), BF16),
            pltpu.SemaphoreType.DMA((9,)),
            pltpu.SemaphoreType.DMA((MESSAGES,)),
            pltpu.SemaphoreType.DMA((MESSAGES,)),
        ],
        compiler_params=pltpu.CompilerParams(
            collective_id=0, has_side_effects=True, vmem_limit_bytes=64 << 20
        ),
        name="transcoder",
    )(
        token_ids.reshape(1, 128),
        enc_bias,
        dec_bias,
        jnp.transpose(incoming, (2, 0, 1)),
        target[0].T,
        returned[0].T,
        cache[0],
        enc_weight[0],
        weights,
    )
    err, out, grad = pl.pallas_call(
        hand_over,
        out_shape=shapes,
        in_specs=[left] * 3,
        out_specs=(left, left, left),
        scratch_shapes=[pltpu.SemaphoreType.DMA((3,))],
        compiler_params=pltpu.CompilerParams(vmem_limit_bytes=64 << 20),
        name="results",
    )(*results)
    return (err.T[None], jnp.transpose(out, (1, 2, 0)), grad[None])


def solution(mesh):
    placed = (
        P("section", None, None),
        P(),
        P("section", ("dp", "tensor"), None),
        P("section", ("dp", "tensor")),
        P("section", None, ("dp", "tensor"), None),
        P("section", ("dp", "tensor")),
        P("section", None, ("dp", "tensor")),
        P("section", None, ("dp", "tensor")),
        P("section", None, ("dp", "tensor")),
    )
    return jax.shard_map(
        local,
        mesh=mesh,
        in_specs=placed,
        out_specs=(
            P("section", None, ("dp", "tensor")),
            P("section", None, ("dp", "tensor")),
            P("section", ("dp", "tensor"), None),
        ),
        check_vma=False,
    )
```
